256 devices in a mesh: tm: 16 (over x, y), space: 16 (over z, core).
Axes of the slice: x: 4, y: 4, z: 8, core: 2. Of those that a mesh axis runs over, the one named last changes fastest.
Arguments:
- fields: bfloat16 [16384, 2, 32768], P('tm', None, 'space')
- calendar_day: int32 [16384], P('tm'), may hold values from 0 to 364, as said below
- events: int32 [16, 96], replicated, may hold values from 0 to 16368, as said below
- lag_offsets: int32 [16], replicated, may hold values from 0 to 15, each once
Outputs:
- composite: float32 [16, 16, 2, 32768], P('tm', None, None, 'space')
The draws below stay inside these ranges and needn't reach their ends.
Inputs may be any that keep to these rules, and one draw needn't show every extreme that they name: `calendar_day`: days of the year of successive record days, one or two calendar days apart. `events`: each entry is a record day; a day may repeat within a type. `lag_offsets`: each of 0 to 15 once.
All inputs are finite; a program needn't handle non-finite values.
Results may differ from the reference program's by a relative error of at most 0.0012.
Values may be sent and summed in bfloat16 or wider, within the bound.
No kernel may reach another device: no remote copies, remote signals or barrier semaphores. Data moves between devices by JAX's collectives and lax.ppermute only.
A program may use at most 64 MiB of HBM per device.

```python
import jax
import jax.numpy as jnp
from jax import lax

TYPES = 16
LAGS = 16
MEMBERS = 96
HARMONICS = 4
DAYS = 16384
POINTS = 32768


TWO_PI = 6.283185307179586


def calendar_draw(key):
    day_steps = jax.random.randint(jax.random.fold_in(key, 11), (DAYS,), 1, 3)
    first_day = jax.random.randint(jax.random.fold_in(key, 12), (), 0, 365)
    return jnp.mod(first_day + jnp.cumsum(day_steps), 365).astype(jnp.int32)


def draw_calendar_day(key, part):
    return calendar_draw(key)


def draw_events(key, part):
    early_pick = jax.random.randint(jax.random.fold_in(key, 21), (TYPES, MEMBERS), 0, DAYS - LAGS + 1)
    later_pick = jax.random.randint(jax.random.fold_in(key, 22), (TYPES, MEMBERS), 0, DAYS - LAGS + 1)
    chosen = jnp.minimum(early_pick, later_pick)
    chosen = chosen.at[0, 0].set(DAYS - LAGS).at[1, 0].set(0)
    return chosen.astype(jnp.int32)


def draw_fields(key, part):
    calendar_days = calendar_draw(key)
    phases = calendar_days.astype(jnp.float32) * (TWO_PI / 365.25)
    orders = jnp.arange(1, HARMONICS + 1).astype(jnp.float32)
    angles = phases[:, None] * orders[None, :]
    basis = jnp.concatenate([jnp.cos(angles), jnp.sin(angles)], axis=1)
    subkeys = jax.random.split(jax.random.fold_in(key, 31), 6)
    scaling = jnp.concatenate([orders, orders])
    amplitudes = jax.random.normal(subkeys[0], (2 * HARMONICS, 2 * POINTS), jnp.float32) * 1.5 / scaling[:, None]
    seasonal = jnp.dot(basis, amplitudes, precision=lax.Precision.HIGHEST)
    position = (jnp.arange(2 * POINTS) % POINTS).astype(jnp.float32) / POINTS
    ramp_factor = 1.0 + 2.0 * position
    levels = jax.random.uniform(subkeys[1], (2 * POINTS,), jnp.float32, 0.5, 1.5) * ramp_factor
    offset = jax.random.normal(subkeys[2], (2 * POINTS,), jnp.float32) * 3.0
    fraction = jnp.arange(DAYS).astype(jnp.float32) / DAYS
    noise_part = jax.random.normal(subkeys[3], (DAYS, 2 * POINTS), jnp.float32) * 0.8
    combined = seasonal + offset[None, :] + 2.0 * fraction[:, None] * levels[None, :] + noise_part * ramp_factor[None, :]
    return combined.reshape(DAYS, 2, POINTS).astype(jnp.bfloat16)


def setup_inputs(seed: int = 0) -> dict:
    streams_of = jax.random.split(jax.random.key(seed), 5)
    return {
        "fields": draw_fields(jax.random.fold_in(streams_of[4], 71), 0),
        "calendar_day": draw_calendar_day(jax.random.fold_in(streams_of[4], 71), 0),
        "events": draw_events(jax.random.fold_in(streams_of[4], 71), 0),
        "lag_offsets": jax.random.permutation(streams_of[3], LAGS).astype(jnp.int32),
    }


TWO_PI = 6.283185307179586

def regressors(calendar_day):
    phases = calendar_day.astype(jnp.float32) * (TWO_PI / 365.25)
    columns = [jnp.ones_like(phases)]
    for harmonic in range(1, HARMONICS + 1):
        columns.append(jnp.cos(harmonic * phases))
        columns.append(jnp.sin(harmonic * phases))
    return jnp.stack(columns, axis=1).astype(jnp.bfloat16)

def solve_fit(gram_matrix, projection):
    factor = jnp.linalg.cholesky(gram_matrix)
    return jax.scipy.linalg.cho_solve((factor, True), projection)

def reference(fields, calendar_day, events, lag_offsets):
    design = regressors(calendar_day)
    record = fields.reshape(DAYS, 2 * POINTS)
    gram_matrix = jnp.dot(design.T.astype(jnp.float32), design.astype(jnp.float32), preferred_element_type=jnp.float32)
    projection = jnp.dot(design.T.astype(jnp.float32), record.astype(jnp.float32), preferred_element_type=jnp.float32)
    coefficients = solve_fit(gram_matrix, projection)
    design_wide = design.astype(jnp.float32)

    def type_sums(event_row):
        chosen = (event_row[:, None] + lag_offsets[None, :]).astype(jnp.int32).reshape(-1)
        picked = jnp.take(record, chosen, axis=0).reshape(MEMBERS, LAGS, 2 * POINTS)
        raw_sums = jnp.sum(picked.astype(jnp.float32), axis=0)
        picked_design = jnp.take(design_wide, chosen, axis=0).reshape(MEMBERS, LAGS, 2 * HARMONICS + 1)
        counted_design = jnp.sum(picked_design, axis=0)
        return raw_sums - jnp.dot(counted_design, coefficients, precision=lax.Precision.HIGHEST)
    totals = lax.map(type_sums, events)
    maps = (totals / MEMBERS).reshape(TYPES, LAGS, 2, POINTS)
    map_mean = jnp.sum(maps, axis=3, keepdims=True) / POINTS
    return maps - map_mean
```

```python
import jax
import jax.numpy as jnp
from jax import lax
from jax.experimental import pallas as pl
from jax.experimental.pallas import tpu as pltpu
from jax.sharding import PartitionSpec as P

HARMONICS = 4
TWO_PI = 6.283185307179586
TERMS = 2 * HARMONICS + 1
SIDE = 4
TILE = 16
EXTRA = 128
F32 = jnp.float32
BF16 = jnp.bfloat16


def iota(shape, axis):
    return lax.broadcasted_iota(jnp.int32, shape, axis)


def dot(a, b):
    return jnp.dot(a, b, preferred_element_type=F32)


def dot_nt(a, b):
    return lax.dot_general(a, b, (((1,), (1,)), ((), ())), preferred_element_type=F32)


def design_rows(days):
    count = days.shape[1]
    phases = days.astype(F32) * (TWO_PI / 365.25)
    row = iota((TILE, count), 0)
    angles = ((row + 1) // 2).astype(F32) * phases
    waves = jnp.where(row % 2 == 1, jnp.cos(angles), jnp.sin(angles))
    rows = jnp.where(row == 0, 1.0, jnp.where(row < TERMS, waves, 0.0))
    return rows.astype(BF16)


def left_factor(me, events_ref, days_ref, left_ref):
    types, members = events_ref.shape
    lags = TILE
    local_days = days_ref.shape[1]
    rows = types * lags
    window = local_days + 128
    events = events_ref[...] - (me * local_days - 128)
    spot = iota((types, window), 1)
    histogram = jnp.zeros((types, window), F32)
    for m in range(members):
        histogram = histogram + jnp.where(events[:, m : m + 1] == spot, 1.0, 0.0)
    counts = jnp.concatenate(
        [histogram[:, 128 - o : 128 - o + local_days].astype(BF16) for o in range(lags)], axis=0
    )
    design = design_rows(days_ref[...])
    out_row = iota((rows, rows), 0)
    in_row = iota((rows, rows), 1)
    first, second, lag = out_row // (SIDE * lags), out_row // lags % SIDE, out_row % lags
    for v in range(2):
        rank = first * SIDE + second if v == 0 else second * SIDE + first
        order = (in_row == lag * types + (rank ^ me)).astype(F32).astype(BF16)
        spread = (iota((128, 256), 1) == 2 * iota((128, 256), 0) + v).astype(F32).astype(BF16)
        top = v * (rows + TILE)
        ordered = dot(order, counts).astype(BF16)
        for b in range(local_days // 128):
            day = slice(128 * b, 128 * b + 128)
            to = slice(256 * b, 256 * b + 256)
            left_ref[top : top + rows, to] = dot(ordered[:, day], spread).astype(BF16)
            left_ref[top + rows : top + rows + TILE, to] = dot(design[:, day], spread).astype(BF16)


def products_kernel(me_ref, events_ref, days_ref, fields_ref, *refs):
    outs, left_ref = refs[:-1], refs[-1]
    step = pl.program_id(0)
    width = fields_ref.shape[2]
    points = outs[0].shape[1] - EXTRA
    group = outs[0].shape[0] - TILE
    rows = SIDE * group

    def put(value, columns):
        for v in range(2):
            top = v * (rows + TILE)
            for r in range(SIDE):
                out = outs[SIDE * v + r]
                out[:group, columns] = value[top + group * r : top + group * (r + 1)]
                out[group:, columns] = value[top + rows : top + rows + TILE]

    @pl.when(step == 0)
    def _():
        left_factor(me_ref[0], events_ref, days_ref, left_ref)
        halves = []
        for v in range(2):
            left = left_ref[v * (rows + TILE) : (v + 1) * (rows + TILE), :]
            design = left[rows:, :]
            pad = jnp.zeros((EXTRA - TILE, left.shape[1]), BF16)
            halves.append(dot_nt(left, jnp.concatenate([design, pad], axis=0)))
        put(jnp.concatenate(halves, axis=0), slice(points, points + EXTRA))

    record = fields_ref.reshape(2 * fields_ref.shape[0], width)[...]
    put(dot(left_ref[...], record), pl.ds(pl.multiple_of(step * width, width), width))


def products(me, events, days, fields):
    local_days, _, points = fields.shape
    types = events.shape[0]
    group = types * TILE // SIDE
    width = 512
    columns = points + EXTRA
    message = jax.ShapeDtypeStruct((group + TILE, columns), F32)
    whole = pl.BlockSpec((group + TILE, columns), lambda i, me: (0, 0), pipeline_mode=pl.Buffered(1))
    return pl.pallas_call(
        products_kernel,
        grid_spec=pltpu.PrefetchScalarGridSpec(
            num_scalar_prefetch=1,
            grid=(points // width,),
            in_specs=[
                pl.BlockSpec(events.shape, lambda i, me: (0, 0)),
                pl.BlockSpec((1, local_days), lambda i, me: (0, 0)),
                pl.BlockSpec((local_days, 2, width), lambda i, me: (0, 0, i)),
            ],
            out_specs=[whole] * (2 * SIDE),
            scratch_shapes=[pltpu.VMEM((2 * (types * TILE + TILE), 2 * local_days), BF16)],
        ),
        out_shape=[message] * (2 * SIDE),
        name="products",
    )(me, events, days.reshape(1, local_days), fields)


def merge_kernel(*refs):
    taken, outs = refs[:SIDE], refs[SIDE:]
    total = taken[0][...]
    for t in taken[1:]:
        total = total + t[...]
    last = total.shape[0] - TILE
    for r, out in enumerate(outs):
        out[:TILE, :] = total[TILE * r : TILE * (r + 1)]
        out[TILE:, :] = total[last:]


def merge(taken):
    columns = taken[0].shape[1]
    out = jax.ShapeDtypeStruct((2 * TILE, columns), F32)
    return pl.pallas_call(merge_kernel, out_shape=[out] * SIDE, name="merge")(*taken)


def finish_kernel(members, lags_ref, *refs):
    taken, (maps_ref, sums_ref, rows_ref) = refs[: 2 * SIDE], refs[2 * SIDE :]
    lags, _, points = maps_ref.shape
    for v in range(2):
        total = taken[SIDE * v][...]
        for t in taken[SIDE * v + 1 : SIDE * (v + 1)]:
            total = total + t[...]
        row = iota((2 * TILE, 1), 0)
        for k in range(TERMS):
            pivot = total[TILE + k : TILE + k + 1, :]
            column = points + k
            factor = total[:, column : column + 1] / pivot[:, column : column + 1]
            factor = jnp.where((row < TILE) | (row > TILE + k), factor, 0.0)
            total = total - factor * pivot
        rows_ref[...] = total[:TILE, :points] / members
        for l in range(lags):
            line = rows_ref[pl.ds(lags_ref[l], 1), :]
            maps_ref[l, v : v + 1, :] = line
            sums_ref[l, v : v + 1, :] = jnp.broadcast_to(jnp.sum(line, axis=1, keepdims=True), (1, 128))


def finish(members, lag_offsets, taken):
    points = taken[0].shape[1] - EXTRA
    lags = lag_offsets.shape[0]
    return pl.pallas_call(
        lambda *refs: finish_kernel(members, *refs),
        grid_spec=pltpu.PrefetchScalarGridSpec(
            num_scalar_prefetch=1,
            grid=(1,),
            in_specs=[pl.BlockSpec(t.shape, lambda i, lags: (0, 0)) for t in taken],
            out_specs=[
                pl.BlockSpec((lags, 2, points), lambda i, lags: (0, 0, 0)),
                pl.BlockSpec((lags, 2, 128), lambda i, lags: (0, 0, 0)),
            ],
            scratch_shapes=[pltpu.VMEM((TILE, points), F32)],
        ),
        out_shape=[
            jax.ShapeDtypeStruct((lags, 2, points), F32),
            jax.ShapeDtypeStruct((lags, 2, 128), F32),
        ],
        name="finish",
    )(lag_offsets, *taken)


def swap(value, axis, mask):
    return lax.ppermute(value, axis, [(i, i ^ mask) for i in range(lax.axis_size(axis))])


def shards(fields, calendar_day, events, lag_offsets):
    me = lax.axis_index("tm").astype(jnp.int32).reshape(1)
    points = fields.shape[2]
    sent = products(me, events, calendar_day, fields)
    mine = [[sent[0]] + [None] * 3, [sent[SIDE]] + [None] * 3]
    for r in (2, 1, 3):
        mine[0][r] = swap(sent[r], "tm", SIDE * r)
        mine[1][r] = swap(sent[SIDE + r], "tm", r)
    taken = []
    for v in range(2):
        parts = merge(mine[v])
        taken += [parts[0]] + [swap(parts[r], "tm", r if v == 0 else SIDE * r) for r in (1, 2, 3)]
    maps, sums = finish(events.shape[1], lag_offsets, taken)
    for mask in (1, 2, 6, 14):
        sums = sums + swap(sums, "space", mask)
    mean = sums[:, :, :1] / (points * lax.axis_size("space"))
    return (maps - mean)[None]


def solution(mesh):
    return jax.shard_map(
        shards,
        mesh=mesh,
        in_specs=(P("tm", None, "space"), P("tm"), P(), P()),
        out_specs=P("tm", None, None, "space"),
        check_vma=False,
    )
```

```python
import jax
import jax.numpy as jnp
from jax import lax
from jax.experimental import pallas as pl
from jax.experimental.pallas import tpu as pltpu
from jax.sharding import PartitionSpec as P

HARMONICS = 4
TWO_PI = 6.283185307179586
TERMS = 2 * HARMONICS + 1
SIDE = 4
TILE = 16
EXTRA = 128
CODE = 32
TOP = 32767.0
SECOND = 65534.0
F32 = jnp.float32
BF16 = jnp.bfloat16


def iota(shape, axis):
    return lax.broadcasted_iota(jnp.int32, shape, axis)


def dot(a, b):
    return jnp.dot(a, b, preferred_element_type=F32)


def dot_nt(a, b):
    return lax.dot_general(a, b, (((1,), (1,)), ((), ())), preferred_element_type=F32)


def design_rows(days):
    count = days.shape[1]
    phases = days.astype(F32) * (TWO_PI / 365.25)
    row = iota((TILE, count), 0)
    angles = ((row + 1) // 2).astype(F32) * phases
    waves = jnp.where(row % 2 == 1, jnp.cos(angles), jnp.sin(angles))
    rows = jnp.where(row == 0, 1.0, jnp.where(row < TERMS, waves, 0.0))
    return rows.astype(BF16)


def left_factor(me, events_ref, days_ref, left_ref):
    types, members = events_ref.shape
    lags = TILE
    local_days = days_ref.shape[1]
    rows = types * lags
    window = local_days + 128
    events = events_ref[...] - (me * local_days - 128)
    spot = iota((types, window), 1)
    histogram = jnp.zeros((types, window), F32)
    for m in range(members):
        histogram = histogram + jnp.where(events[:, m : m + 1] == spot, 1.0, 0.0)
    counts = jnp.concatenate(
        [histogram[:, 128 - o : 128 - o + local_days].astype(BF16) for o in range(lags)], axis=0
    )
    design = design_rows(days_ref[...])
    out_row = iota((rows, rows), 0)
    in_row = iota((rows, rows), 1)
    first, second, lag = out_row // (SIDE * lags), out_row // lags % SIDE, out_row % lags
    for v in range(2):
        rank = first * SIDE + second if v == 0 else second * SIDE + first
        order = (in_row == lag * types + (rank ^ me)).astype(F32).astype(BF16)
        spread = (iota((128, 256), 1) == 2 * iota((128, 256), 0) + v).astype(F32).astype(BF16)
        top = v * (rows + TILE)
        ordered = dot(order, counts).astype(BF16)
        for b in range(local_days // 128):
            day = slice(128 * b, 128 * b + 128)
            to = slice(256 * b, 256 * b + 256)
            left_ref[top : top + rows, to] = dot(ordered[:, day], spread).astype(BF16)
            left_ref[top + rows : top + rows + TILE, to] = dot(design[:, day], spread).astype(BF16)


def lane_sum(block):
    parts = [block[:, c : c + 128] for c in range(0, block.shape[1], 128)]
    while len(parts) > 1:
        parts = [x + y for x, y in zip(parts[::2], parts[1::2])] + parts[len(parts) & ~1 :]
    return parts[0]


def to_words(value, unit):
    scaled = value * unit
    high = jnp.round(scaled)
    return high, jnp.round((scaled - high) * SECOND)


def row_unit(code):
    return jnp.exp2(code * (-1.0 / 16.0)) * TOP


def row_code(value):
    peak = jnp.max(jnp.abs(value), axis=1, keepdims=True)
    return jnp.ceil(16.0 * jnp.log2(jnp.maximum(peak, 1e-30))) + 1.0


def to_int16(value):
    return jnp.clip(value, -TOP, TOP).astype(jnp.int32).astype(jnp.int16)


def encode(out, main, aux, members, total_days):
    rows, points = main.shape[0], main.shape[1] - EXTRA
    lane = iota((1, EXTRA), 1)

    def extra(block, code, unit):
        high, low = to_words(block, unit)
        low = jnp.where((lane >= TILE) & (lane < 2 * TILE), pltpu.roll(low, TILE, 1), 0.0)
        return to_int16(jnp.where(lane < TILE, high, low) + jnp.where(lane == CODE, code, 0.0))

    constant = aux[0:1, :points]
    mean = constant / aux[0:1, points : points + 1]
    centred = main[:, :points] - main[:, points : points + 1] * mean
    code = row_code(centred)
    out[:rows, :points] = to_int16(jnp.round(centred * row_unit(code)))
    out[:rows, points:] = extra(main[:, points:], code, TOP / members)
    row = iota((TILE, 1), 0)
    harmonic = aux[:, :points] - aux[:, points : points + 1] * mean
    harmonic = jnp.where(row == 0, constant, harmonic)
    code = row_code(harmonic)
    high, low = to_words(constant, row_unit(code[0:1]))
    words = jnp.where(row == 0, high, jnp.round(harmonic * row_unit(code)))
    out[rows:, :points] = to_int16(jnp.where(row == TERMS, low, words))
    out[rows:, points:] = extra(aux[:, points:], code, TOP / total_days)


def decode(message, members, total_days):
    rows, points = message.shape[0] - TILE, message.shape[1] - EXTRA
    lane = iota((1, EXTRA), 1)

    def extra(block, unit):
        words = block + pltpu.roll(block, EXTRA - TILE, 1) * (1.0 / SECOND)
        return jnp.where(lane < TILE, words * (1.0 / unit), 0.0)

    def values(block):
        block = block.astype(jnp.int32).astype(F32)
        code = block[:, points + CODE : points + CODE + 1]
        return block[:, :points], block[:, points:], jnp.exp2(code * (1.0 / 16.0)) * (1.0 / TOP)

    words, behind, step = values(message[rows:])
    low_side = extra(behind, TOP / total_days)
    constant = (words[0:1] + words[TERMS : TERMS + 1] * (1.0 / SECOND)) * step[0:1]
    mean = constant / low_side[0:1, 0:1]
    row = iota((TILE, 1), 0)
    aux = words * step + low_side[:, 0:1] * mean
    aux = jnp.where(row == 0, constant, jnp.where(row < TERMS, aux, 0.0))
    words, behind, step = values(message[:rows])
    side = extra(behind, TOP / members)
    return words * step + side[:, 0:1] * mean, side, aux, low_side


def products_kernel(total_days, me_ref, events_ref, days_ref, fields_ref, *refs):
    outs, sums_ref, (left_ref, all_ref) = refs[:-3], refs[-3], refs[-2:]
    step = pl.program_id(0)
    width = fields_ref.shape[2]
    members = events_ref.shape[1]
    points = outs[0].shape[1] - EXTRA
    group = outs[0].shape[0] - TILE
    rows = SIDE * group
    half = rows + TILE

    @pl.when(step == 0)
    def _():
        left_factor(me_ref[0], events_ref, days_ref, left_ref)
        for v in range(2):
            left = left_ref[v * half : (v + 1) * half, :]
            pad = jnp.zeros((EXTRA - TILE, left.shape[1]), BF16)
            all_ref[v * half : (v + 1) * half, points:] = dot_nt(
                left, jnp.concatenate([left[rows:, :], pad], axis=0)
            )

    record = fields_ref.reshape(2 * fields_ref.shape[0], width)[...]
    columns = pl.ds(pl.multiple_of(step * width, width), width)
    all_ref[:, columns] = dot(left_ref[...], record)

    @pl.when(step == pl.num_programs(0) - 1)
    def _():
        for r in (2, 1, 3, 0):
            for v in range(2):
                top = v * half + group * r
                out = outs[SIDE * v + r]
                if r:
                    main = all_ref[top : top + group, :]
                    aux = all_ref[v * half + rows : (v + 1) * half, :]
                    encode(out, main, aux, members, total_days)
                else:
                    out[:group, :] = all_ref[top : top + group, :]
                    out[group:, :] = all_ref[v * half + rows : (v + 1) * half, :]
        partial = []
        for i in range(SIDE * SIDE):
            for v in range(2):
                place = i if v == 0 else i % SIDE * SIDE + i // SIDE
                top = v * half + TILE * place
                partial.append(lane_sum(all_ref[top : top + TILE, :points]))
        for v in range(2):
            partial.append(lane_sum(all_ref[v * half + rows : (v + 1) * half, :points]))
        sums_ref[...] = lax.dot_general(
            jnp.ones((8, 128), F32),
            jnp.concatenate(partial, axis=0),
            (((1,), (1,)), ((), ())),
            precision=lax.Precision.HIGHEST,
            preferred_element_type=F32,
        )


def products(me, events, days, fields):
    local_days, _, points = fields.shape
    types = events.shape[0]
    group = types * TILE // SIDE
    half = types * TILE + TILE
    width = 512
    columns = points + EXTRA
    kept = jax.ShapeDtypeStruct((group + TILE, columns), F32)
    message = jax.ShapeDtypeStruct((group + TILE, columns), jnp.int16)
    once = dict(pipeline_mode=pl.Buffered(1))
    whole = pl.BlockSpec((group + TILE, columns), lambda i, me: (0, 0), **once)
    total_days = local_days * lax.axis_size("tm")
    return pl.pallas_call(
        lambda *refs: products_kernel(total_days, *refs),
        grid_spec=pltpu.PrefetchScalarGridSpec(
            num_scalar_prefetch=1,
            grid=(points // width,),
            in_specs=[
                pl.BlockSpec(events.shape, lambda i, me: (0, 0)),
                pl.BlockSpec((1, local_days), lambda i, me: (0, 0)),
                pl.BlockSpec((local_days, 2, width), lambda i, me: (0, 0, i)),
            ],
            out_specs=[whole] * (2 * SIDE) + [pl.BlockSpec((8, 2 * half), lambda i, me: (0, 0), **once)],
            scratch_shapes=[
                pltpu.VMEM((2 * half, 2 * local_days), BF16),
                pltpu.VMEM((2 * half, columns), F32),
            ],
        ),
        out_shape=([kept] + [message] * (SIDE - 1)) * 2 + [jax.ShapeDtypeStruct((8, 2 * half), F32)],
        name="products",
    )(me, events, days.reshape(1, local_days), fields)


def added(taken, members, total_days):
    rows, points = taken[0].shape[0] - TILE, taken[0].shape[1] - EXTRA
    kept = taken[0]
    main, side = kept[:rows, :points], kept[:rows, points:]
    aux, low_side = kept[rows:, :points], kept[rows:, points:]
    for t in taken[1:]:
        a, b, c, d = decode(t, members, total_days)
        main, side, aux, low_side = main + a, side + b, aux + c, low_side + d
    main = jnp.concatenate([main, side], axis=1)
    aux = jnp.concatenate([aux, low_side], axis=1)
    return main, aux


def merge_kernel(members, total_days, *refs):
    taken, outs = refs[:SIDE], refs[SIDE:]
    main, aux = added(taken, members, total_days)
    for r in (2, 1, 3):
        encode(outs[r], main[TILE * r : TILE * (r + 1)], aux, members, total_days)
    outs[0][:TILE, :] = main[:TILE]
    outs[0][TILE:, :] = aux


def merge(taken, members, total_days):
    columns = taken[0].shape[1]
    kept = jax.ShapeDtypeStruct((2 * TILE, columns), F32)
    message = jax.ShapeDtypeStruct((2 * TILE, columns), jnp.int16)
    return pl.pallas_call(
        lambda *refs: merge_kernel(members, total_days, *refs),
        out_shape=[kept] + [message] * (SIDE - 1),
        name="merge",
    )(*taken)


def finish_kernel(members, total_days, all_points, lags_ref, sums_ref, *refs):
    taken, (maps_ref, rows_ref) = refs[: 2 * SIDE], refs[2 * SIDE :]
    lags, _, points = maps_ref.shape
    for v in range(2):
        total = jnp.concatenate(added(taken[SIDE * v : SIDE * (v + 1)], members, total_days), axis=0)
        row, lane = iota((2 * TILE, 1), 0), iota((1, EXTRA), 1)
        place = jnp.where(row < TILE, row + TILE * v, row + TILE * (v + 1))
        over = jnp.where(iota((1, 4 * TILE), 1) == place, sums_ref[0:1, :], 0.0)
        over = jnp.sum(over, axis=1, keepdims=True)
        side = jnp.where(lane == CODE, over, total[:, points:])
        total = jnp.concatenate([total[:, :points], side], axis=1)
        for k in range(TERMS):
            pivot = total[TILE + k : TILE + k + 1, :]
            column = points + k
            factor = total[:, column : column + 1] / pivot[:, column : column + 1]
            factor = jnp.where((row < TILE) | (row > TILE + k), factor, 0.0)
            total = total - factor * pivot
        column = points + CODE
        mean = total[:TILE, column : column + 1] / all_points
        rows_ref[...] = (total[:TILE, :points] - mean) / members
        for l in range(lags):
            maps_ref[l, v : v + 1, :] = rows_ref[pl.ds(lags_ref[l], 1), :]


def finish(members, total_days, all_points, lag_offsets, sums, taken):
    points = taken[0].shape[1] - EXTRA
    lags = lag_offsets.shape[0]
    return pl.pallas_call(
        lambda *refs: finish_kernel(members, total_days, all_points, *refs),
        grid_spec=pltpu.PrefetchScalarGridSpec(
            num_scalar_prefetch=1,
            grid=(1,),
            in_specs=[pl.BlockSpec(t.shape, lambda i, lags: (0, 0)) for t in [sums, *taken]],
            out_specs=pl.BlockSpec((lags, 2, points), lambda i, lags: (0, 0, 0)),
            scratch_shapes=[pltpu.VMEM((TILE, points), F32)],
        ),
        out_shape=jax.ShapeDtypeStruct((lags, 2, points), F32),
        name="finish",
    )(lag_offsets, sums, *taken)


def swap(value, axis, mask):
    return lax.ppermute(value, axis, [(i, i ^ mask) for i in range(lax.axis_size(axis))])


def map_sums(sums):
    own, design = sums[:1, : -2 * TILE], sums[:1, -2 * TILE :]
    mask = SIDE * SIDE // 2
    while mask:
        middle = own.shape[1] // 2
        got = swap(jnp.concatenate([own[:, middle:], design], axis=1), "tm", mask)
        own, design = own[:, :middle] + got[:, :middle], design + got[:, middle:]
        mask //= 2
    total = jnp.concatenate([own, design], axis=1)
    for mask in (1, 2, 6, 14):
        total = total + swap(total, "space", mask)
    return jnp.broadcast_to(total, (8, total.shape[1]))


def shards(fields, calendar_day, events, lag_offsets):
    me = lax.axis_index("tm").astype(jnp.int32).reshape(1)
    members = events.shape[1]
    total_days = fields.shape[0] * lax.axis_size("tm")
    all_points = fields.shape[2] * lax.axis_size("space")
    *sent, sums = products(me, events, calendar_day, fields)
    mine = [[sent[0]] + [None] * 3, [sent[SIDE]] + [None] * 3]
    for r in (2, 1, 3):
        mine[0][r] = swap(sent[r], "tm", SIDE * r)
        mine[1][r] = swap(sent[SIDE + r], "tm", r)
    sums = map_sums(sums)
    taken = []
    for v in range(2):
        parts = merge(mine[v], members, total_days)
        taken += [parts[0]] + [swap(parts[r], "tm", r if v == 0 else SIDE * r) for r in (1, 2, 3)]
    return finish(members, total_days, all_points, lag_offsets, sums, taken)[None]


def solution(mesh):
    return jax.shard_map(
        shards,
        mesh=mesh,
        in_specs=(P("tm", None, "space"), P("tm"), P(), P()),
        out_specs=P("tm", None, None, "space"),
        check_vma=False,
    )
```

```python
import jax
import jax.numpy as jnp
from jax import lax
from jax.experimental import pallas as pl
from jax.experimental.pallas import tpu as pltpu
from jax.sharding import PartitionSpec as P

HARMONICS = 4
TWO_PI = 6.283185307179586
TERMS = 2 * HARMONICS + 1
SIDE = 4
TILE = 16
EXTRA = 128
CODE = 32
MERGE_VMEM, PRODUCTS_VMEM = 16 << 20, 40 << 20
CHUNK = 512
TOP = 32767.0
SECOND = 65534.0
F32 = jnp.float32
BF16 = jnp.bfloat16


def iota(shape, axis):
    return lax.broadcasted_iota(jnp.int32, shape, axis)


def dot(a, b):
    return jnp.dot(a, b, preferred_element_type=F32)


def dot_nt(a, b):
    return lax.dot_general(a, b, (((1,), (1,)), ((), ())), preferred_element_type=F32)


def design_rows(days):
    count = days.shape[1]
    phases = days.astype(F32) * (TWO_PI / 365.25)
    row = iota((TILE, count), 0)
    angles = ((row + 1) // 2).astype(F32) * phases
    waves = jnp.where(row % 2 == 1, jnp.cos(angles), jnp.sin(angles))
    rows = jnp.where(row == 0, 1.0, jnp.where(row < TERMS, waves, 0.0))
    return rows.astype(BF16)


def left_factor(me, events_ref, days_ref, left_ref):
    types, members = events_ref.shape
    lags = TILE
    local_days = days_ref.shape[1]
    rows = types * lags
    window = local_days + 128
    events = events_ref[...] - (me * local_days - 128)
    spot = iota((types, window), 1)
    histogram = jnp.zeros((types, window), F32)
    for m in range(members):
        histogram = histogram + jnp.where(events[:, m : m + 1] == spot, 1.0, 0.0)
    counts = jnp.concatenate(
        [histogram[:, 128 - o : 128 - o + local_days].astype(BF16) for o in range(lags)], axis=0
    )
    design = design_rows(days_ref[...])
    out_row = iota((rows, rows), 0)
    in_row = iota((rows, rows), 1)
    first, second, lag = out_row // (SIDE * lags), out_row // lags % SIDE, out_row % lags
    for v in range(2):
        rank = first * SIDE + second if v == 0 else second * SIDE + first
        order = (in_row == lag * types + (rank ^ me)).astype(F32).astype(BF16)
        spread = (iota((128, 256), 1) == 2 * iota((128, 256), 0) + v).astype(F32).astype(BF16)
        top = v * (rows + TILE)
        ordered = dot(order, counts).astype(BF16)
        for b in range(local_days // 128):
            day = slice(128 * b, 128 * b + 128)
            to = slice(256 * b, 256 * b + 256)
            left_ref[top : top + rows, to] = dot(ordered[:, day], spread).astype(BF16)
            left_ref[top + rows : top + rows + TILE, to] = dot(design[:, day], spread).astype(BF16)


def lane_sum(block):
    parts = [block[:, c : c + 128] for c in range(0, block.shape[1], 128)]
    while len(parts) > 1:
        parts = [x + y for x, y in zip(parts[::2], parts[1::2])] + parts[len(parts) & ~1 :]
    return parts[0]


def to_words(value, unit):
    scaled = value * unit
    high = jnp.round(scaled)
    return high, jnp.round((scaled - high) * SECOND)


def row_unit(code):
    return jnp.exp2(code * (-1.0 / 16.0)) * TOP


def row_code(value):
    peak = jnp.max(jnp.abs(value), axis=1, keepdims=True)
    return jnp.ceil(16.0 * jnp.log2(jnp.maximum(peak, 1e-30))) + 1.0


def to_int16(value):
    return value.astype(jnp.int32).astype(jnp.int16)


def encode(out, main, aux, members, total_days):
    rows, points = main.shape[0], main.shape[1] - EXTRA
    lane = iota((1, EXTRA), 1)

    def extra(block, code, unit):
        high, low = to_words(block, unit)
        low = jnp.where((lane >= TILE) & (lane < 2 * TILE), pltpu.roll(low, TILE, 1), 0.0)
        return to_int16(jnp.where(lane < TILE, high, low) + jnp.where(lane == CODE, code, 0.0))

    constant = aux[0:1, :points]
    mean = constant / aux[0:1, points : points + 1]
    centred = main[:, :points] - main[:, points : points + 1] * mean
    code = row_code(centred)
    out[:rows, :points] = to_int16(jnp.round(centred * row_unit(code)))
    out[:rows, points:] = extra(main[:, points:], code, TOP / members)
    row = iota((TILE, 1), 0)
    harmonic = aux[:, :points] - aux[:, points : points + 1] * mean
    harmonic = jnp.where(row == 0, constant, harmonic)
    code = row_code(harmonic)
    high, low = to_words(constant, row_unit(code[0:1]))
    words = jnp.where(row == 0, high, jnp.round(harmonic * row_unit(code)))
    out[rows:, :points] = to_int16(jnp.where(row == TERMS, low, words))
    out[rows:, points:] = extra(aux[:, points:], code, TOP / total_days)


def decode(message, members, total_days):
    rows, points = message.shape[0] - TILE, message.shape[1] - EXTRA
    lane = iota((1, EXTRA), 1)

    def extra(block, unit):
        words = block + pltpu.roll(block, EXTRA - TILE, 1) * (1.0 / SECOND)
        return jnp.where(lane < TILE, words * (1.0 / unit), 0.0)

    def values(block):
        block = block.astype(jnp.int32).astype(F32)
        code = block[:, points + CODE : points + CODE + 1]
        return block[:, :points], block[:, points:], jnp.exp2(code * (1.0 / 16.0)) * (1.0 / TOP)

    words, behind, step = values(message[rows:])
    low_side = extra(behind, TOP / total_days)
    constant = (words[0:1] + words[TERMS : TERMS + 1] * (1.0 / SECOND)) * step[0:1]
    mean = constant / low_side[0:1, 0:1]
    row = iota((TILE, 1), 0)
    aux = words * step + low_side[:, 0:1] * mean
    aux = jnp.where(row == 0, constant, jnp.where(row < TERMS, aux, 0.0))
    words, behind, step = values(message[:rows])
    side = extra(behind, TOP / members)
    return words * step + side[:, 0:1] * mean, side, aux, low_side


def products_kernel(total_days, me_ref, events_ref, days_ref, fields_ref, *refs):
    outs, sums_ref, (record_ref, left_ref, all_ref, part_ref, arrived) = refs[:-6], refs[-6], refs[-5:]
    members = events_ref.shape[1]
    points = fields_ref.shape[2]
    group = outs[0].shape[0] - TILE
    rows = SIDE * group
    half = rows + TILE
    chunks = [slice(c, c + CHUNK) for c in range(0, points, CHUNK)]
    copies = [
        pltpu.make_async_copy(fields_ref.at[:, :, c], record_ref.at[:, :, c], arrived.at[i])
        for i, c in enumerate(chunks)
    ]
    for copy in copies:
        copy.start()
    left_factor(me_ref[0], events_ref, days_ref, left_ref)
    for v in range(2):
        left = left_ref[v * half : (v + 1) * half, :]
        pad = jnp.zeros((EXTRA - TILE, left.shape[1]), BF16)
        all_ref[v * half : (v + 1) * half, points:] = dot_nt(
            left, jnp.concatenate([left[rows:, :], pad], axis=0)
        )
    record = record_ref.reshape(2 * record_ref.shape[0], points)
    for copy, c in zip(copies, chunks):
        copy.wait()
        all_ref[:, c] = dot(left_ref[...], record[:, c])
    for r in (2, 1, 3, 0):
        for v in range(2):
            top = v * half + group * r
            out = outs[SIDE * v + r]
            if r:
                main = all_ref[top : top + group, :]
                aux = all_ref[v * half + rows : (v + 1) * half, :]
                encode(out, main, aux, members, total_days)
            else:
                out[:group, :] = all_ref[top : top + group, :]
                out[group:, :] = all_ref[v * half + rows : (v + 1) * half, :]
    for i in range(SIDE * SIDE):
        for v in range(2):
            place = i if v == 0 else i % SIDE * SIDE + i // SIDE
            top = v * half + TILE * place
            part_ref[2 * TILE * i + TILE * v : 2 * TILE * i + TILE * (v + 1), :] = lane_sum(
                all_ref[top : top + TILE, :points]
            )
    design = [lane_sum(all_ref[v * half + rows : (v + 1) * half, :points]) for v in range(2)]
    types = [
        part_ref[pl.ds(pl.multiple_of((e ^ me_ref[0]) * 2 * TILE, 2 * TILE), 2 * TILE), :]
        for e in range(SIDE * SIDE)
    ]
    totals = lax.dot_general(
        jnp.ones((8, 128), F32),
        jnp.concatenate(types + design, axis=0),
        (((1,), (1,)), ((), ())),
        precision=lax.Precision.HIGHEST,
        preferred_element_type=F32,
    )
    count = 2 * TILE
    last = totals[0:1, count * SIDE * SIDE :]
    space = sums_ref.shape[0] // (SIDE * SIDE)
    for e in range(SIDE * SIDE):
        line = [totals[0:1, count * e : count * (e + 1)], last, jnp.zeros((1, 128 - 2 * count), F32)]
        line = jnp.broadcast_to(jnp.concatenate(line, axis=1), (space, 128))
        sums_ref[space * e : space * (e + 1), :] = line


def vmem():
    return pl.BlockSpec(memory_space=pltpu.VMEM)


def products(me, events, days, fields):
    local_days, _, points = fields.shape
    types = events.shape[0]
    group = types * TILE // SIDE
    half = types * TILE + TILE
    columns = points + EXTRA
    kept = jax.ShapeDtypeStruct((group + TILE, columns), F32)
    message = jax.ShapeDtypeStruct((group + TILE, columns), jnp.int16)
    tm = lax.axis_size("tm")
    sums = jax.ShapeDtypeStruct((tm * lax.axis_size("space"), 128), F32)
    return pl.pallas_call(
        lambda *refs: products_kernel(local_days * tm, *refs),
        in_specs=[
            pl.BlockSpec(memory_space=pltpu.SMEM),
            vmem(),
            vmem(),
            pl.BlockSpec(memory_space=pl.ANY),
        ],
        out_specs=[vmem()] * (2 * SIDE + 1),
        out_shape=([kept] + [message] * (SIDE - 1)) * 2 + [sums],
        scratch_shapes=[
            pltpu.VMEM(fields.shape, BF16),
            pltpu.VMEM((2 * half, 2 * local_days), BF16),
            pltpu.VMEM((2 * half, columns), F32),
            pltpu.VMEM((2 * types * TILE, 128), F32),
            pltpu.SemaphoreType.DMA((points // CHUNK,)),
        ],
        compiler_params=pltpu.CompilerParams(vmem_limit_bytes=PRODUCTS_VMEM),
        name="products",
    )(me, events, days.reshape(1, local_days), fields)


def added(taken, members, total_days):
    rows, points = taken[0].shape[0] - TILE, taken[0].shape[1] - EXTRA
    kept = taken[0]
    main, side = kept[:rows, :points], kept[:rows, points:]
    aux, low_side = kept[rows:, :points], kept[rows:, points:]
    for t in taken[1:]:
        a, b, c, d = decode(t, members, total_days)
        main, side, aux, low_side = main + a, side + b, aux + c, low_side + d
    main = jnp.concatenate([main, side], axis=1)
    aux = jnp.concatenate([aux, low_side], axis=1)
    return main, aux


def merge_kernel(members, total_days, *refs):
    taken, outs = refs[:SIDE], refs[SIDE:]
    main, aux = added(taken, members, total_days)
    for r in (2, 1, 3):
        encode(outs[r], main[TILE * r : TILE * (r + 1)], aux, members, total_days)
    outs[0][:TILE, :] = main[:TILE]
    outs[0][TILE:, :] = aux


def merge(taken, members, total_days):
    columns = taken[0].shape[1]
    kept = jax.ShapeDtypeStruct((2 * TILE, columns), F32)
    message = jax.ShapeDtypeStruct((2 * TILE, columns), jnp.int16)
    return pl.pallas_call(
        lambda *refs: merge_kernel(members, total_days, *refs),
        in_specs=[vmem()] * SIDE,
        out_specs=[vmem()] * SIDE,
        out_shape=[kept] + [message] * (SIDE - 1),
        compiler_params=pltpu.CompilerParams(vmem_limit_bytes=MERGE_VMEM),
        name="merge",
    )(*taken)


def finish_kernel(members, total_days, all_points, lags_ref, sums_ref, *refs):
    taken, (maps_ref, rows_ref) = refs[: 2 * SIDE], refs[2 * SIDE :]
    lags, _, points = maps_ref.shape
    sums = jnp.sum(sums_ref[...], axis=0, keepdims=True)
    for v in range(2):
        total = jnp.concatenate(added(taken[SIDE * v : SIDE * (v + 1)], members, total_days), axis=0)
        row, lane = iota((2 * TILE, 1), 0), iota((1, EXTRA), 1)
        place = jnp.where(row < TILE, row + TILE * v, row + TILE * (v + 1))
        over = jnp.where(iota((1, 128), 1) == place, sums, 0.0)
        over = jnp.sum(over, axis=1, keepdims=True)
        side = jnp.where(lane == CODE, over, total[:, points:])
        total = jnp.concatenate([total[:, :points], side], axis=1)
        for k in range(TERMS):
            pivot = total[TILE + k : TILE + k + 1, :]
            column = points + k
            factor = total[:, column : column + 1] / pivot[:, column : column + 1]
            factor = jnp.where((row < TILE) | (row > TILE + k), factor, 0.0)
            total = total - factor * pivot
        column = points + CODE
        mean = total[:TILE, column : column + 1] / all_points
        rows_ref[...] = (total[:TILE, :points] - mean) / members
        for l in range(lags):
            maps_ref[l, v : v + 1, :] = rows_ref[pl.ds(lags_ref[l], 1), :]


def finish(members, total_days, all_points, lag_offsets, sums, taken):
    points = taken[0].shape[1] - EXTRA
    lags = lag_offsets.shape[0]
    return pl.pallas_call(
        lambda *refs: finish_kernel(members, total_days, all_points, *refs),
        in_specs=[pl.BlockSpec(memory_space=pltpu.SMEM)] + [vmem()] * (2 * SIDE + 1),
        scratch_shapes=[pltpu.VMEM((TILE, points), F32)],
        out_shape=jax.ShapeDtypeStruct((lags, 2, points), F32),
        compiler_params=pltpu.CompilerParams(vmem_limit_bytes=MERGE_VMEM),
        name="finish",
    )(lag_offsets, sums, *taken)


def swap(value, axis, mask):
    return lax.ppermute(value, axis, [(i, i ^ mask) for i in range(lax.axis_size(axis))])


def shards(fields, calendar_day, events, lag_offsets):
    me = lax.axis_index("tm").astype(jnp.int32).reshape(1)
    members = events.shape[1]
    total_days = fields.shape[0] * lax.axis_size("tm")
    all_points = fields.shape[2] * lax.axis_size("space")
    *sent, sums = products(me, events, calendar_day, fields)
    mine = [[sent[0]] + [None] * 3, [sent[SIDE]] + [None] * 3]
    for r in (2, 1, 3):
        mine[0][r] = swap(sent[r], "tm", SIDE * r)
        mine[1][r] = swap(sent[SIDE + r], "tm", r)
    sums = lax.all_to_all(sums, ("tm", "space"), 0, 0, tiled=True)
    taken = []
    for v in range(2):
        parts = merge(mine[v], members, total_days)
        taken += [parts[0]] + [swap(parts[r], "tm", r if v == 0 else SIDE * r) for r in (1, 2, 3)]
    return finish(members, total_days, all_points, lag_offsets, sums, taken)[None]


def solution(mesh):
    return jax.shard_map(
        shards,
        mesh=mesh,
        in_specs=(P("tm", None, "space"), P("tm"), P(), P()),
        out_specs=P("tm", None, None, "space"),
        check_vma=False,
    )
```

```python
import jax
import jax.numpy as jnp
from jax import lax
from jax.experimental import pallas as pl
from jax.experimental.pallas import tpu as pltpu
from jax.sharding import PartitionSpec as P

HARMONICS = 4
TWO_PI = 6.283185307179586
TERMS = 2 * HARMONICS + 1
SIDE = 4
TILE = 16
EXTRA = 128
CODE = 32
MERGE_VMEM, PRODUCTS_VMEM = 8 << 20, 24 << 20
CHUNK = 512
TOP = 32767.0
SECOND = 65534.0
F32 = jnp.float32
BF16 = jnp.bfloat16


def iota(shape, axis):
    return lax.broadcasted_iota(jnp.int32, shape, axis)


def dot(a, b):
    return jnp.dot(a, b, preferred_element_type=F32)


def dot_nt(a, b):
    return lax.dot_general(a, b, (((1,), (1,)), ((), ())), preferred_element_type=F32)


def design_rows(days):
    count = days.shape[1]
    phases = days.astype(F32) * (TWO_PI / 365.25)
    row = iota((TILE, count), 0)
    angles = ((row + 1) // 2).astype(F32) * phases
    waves = jnp.where(row % 2 == 1, jnp.cos(angles), jnp.sin(angles))
    rows = jnp.where(row == 0, 1.0, jnp.where(row < TERMS, waves, 0.0))
    return rows.astype(BF16)


def left_factor(me, events_ref, days_ref, left_ref):
    types, members = events_ref.shape
    lags = TILE
    local_days = days_ref.shape[1]
    rows = types * lags
    window = local_days + 128
    events = events_ref[...] - (me * local_days - 128)
    spot = iota((types, window), 1)
    histogram = jnp.zeros((types, window), F32)
    for m in range(members):
        histogram = histogram + jnp.where(events[:, m : m + 1] == spot, 1.0, 0.0)
    counts = jnp.concatenate(
        [histogram[:, 128 - o : 128 - o + local_days].astype(BF16) for o in range(lags)], axis=0
    )
    design = design_rows(days_ref[...])
    out_row = iota((rows, rows), 0)
    in_row = iota((rows, rows), 1)
    first, second, lag = out_row // (SIDE * lags), out_row // lags % SIDE, out_row % lags
    for v in range(2):
        rank = first * SIDE + second if v == 0 else second * SIDE + first
        order = (in_row == lag * types + (rank ^ me)).astype(F32).astype(BF16)
        spread = (iota((128, 256), 1) == 2 * iota((128, 256), 0) + v).astype(F32).astype(BF16)
        top = v * (rows + TILE)
        ordered = dot(order, counts).astype(BF16)
        for b in range(local_days // 128):
            day = slice(128 * b, 128 * b + 128)
            to = slice(256 * b, 256 * b + 256)
            left_ref[top : top + rows, to] = dot(ordered[:, day], spread).astype(BF16)
            left_ref[top + rows : top + rows + TILE, to] = dot(design[:, day], spread).astype(BF16)


def lane_sum(block):
    parts = [block[:, c : c + 128] for c in range(0, block.shape[1], 128)]
    while len(parts) > 1:
        parts = [x + y for x, y in zip(parts[::2], parts[1::2])] + parts[len(parts) & ~1 :]
    return parts[0]


def to_words(value, unit):
    scaled = value * unit
    high = jnp.round(scaled)
    return high, jnp.round((scaled - high) * SECOND)


def row_unit(code):
    return jnp.exp2(code * (-1.0 / 16.0)) * TOP


def row_code(value):
    peak = jnp.max(jnp.abs(value), axis=1, keepdims=True)
    return jnp.ceil(16.0 * jnp.log2(jnp.maximum(peak, 1e-30))) + 1.0


def to_int16(value):
    return value.astype(jnp.int32).astype(jnp.int16)


def encode(out, main, aux, members, total_days):
    rows, points = main.shape[0], main.shape[1] - EXTRA
    lane = iota((1, EXTRA), 1)

    def extra(block, code, unit):
        high, low = to_words(block, unit)
        low = jnp.where((lane >= TILE) & (lane < 2 * TILE), pltpu.roll(low, TILE, 1), 0.0)
        return to_int16(jnp.where(lane < TILE, high, low) + jnp.where(lane == CODE, code, 0.0))

    constant = aux[0:1, :points]
    mean = constant / aux[0:1, points : points + 1]
    centred = main[:, :points] - main[:, points : points + 1] * mean
    code = row_code(centred)
    out[:rows, :points] = to_int16(jnp.round(centred * row_unit(code)))
    out[:rows, points:] = extra(main[:, points:], code, TOP / members)
    row = iota((TILE, 1), 0)
    harmonic = aux[:, :points] - aux[:, points : points + 1] * mean
    harmonic = jnp.where(row == 0, constant, harmonic)
    code = row_code(harmonic)
    high, low = to_words(constant, row_unit(code[0:1]))
    words = jnp.where(row == 0, high, jnp.round(harmonic * row_unit(code)))
    out[rows:, :points] = to_int16(jnp.where(row == TERMS, low, words))
    out[rows:, points:] = extra(aux[:, points:], code, TOP / total_days)


def decode(message, members, total_days):
    rows, points = message.shape[0] - TILE, message.shape[1] - EXTRA
    lane = iota((1, EXTRA), 1)

    def extra(block, unit):
        words = block + pltpu.roll(block, EXTRA - TILE, 1) * (1.0 / SECOND)
        return jnp.where(lane < TILE, words * (1.0 / unit), 0.0)

    def values(block):
        block = block.astype(jnp.int32).astype(F32)
        code = block[:, points + CODE : points + CODE + 1]
        return block[:, :points], block[:, points:], jnp.exp2(code * (1.0 / 16.0)) * (1.0 / TOP)

    words, behind, step = values(message[rows:])
    low_side = extra(behind, TOP / total_days)
    constant = (words[0:1] + words[TERMS : TERMS + 1] * (1.0 / SECOND)) * step[0:1]
    mean = constant / low_side[0:1, 0:1]
    row = iota((TILE, 1), 0)
    aux = words * step + low_side[:, 0:1] * mean
    aux = jnp.where(row == 0, constant, jnp.where(row < TERMS, aux, 0.0))
    words, behind, step = values(message[:rows])
    side = extra(behind, TOP / members)
    return words * step + side[:, 0:1] * mean, side, aux, low_side


def products_kernel(total_days, me_ref, events_ref, days_ref, fields_ref, *refs):
    outs, sums_ref = refs[:-8], refs[-8]
    record_ref, left_ref, all_ref, part_ref, own_events, own_days, arrived = refs[-7:]
    members = events_ref.shape[1]
    points = fields_ref.shape[2]
    group = outs[0].shape[0] - TILE
    rows = SIDE * group
    half = rows + TILE
    chunks = [slice(c, c + CHUNK) for c in range(0, points, CHUNK)]
    copies = [
        pltpu.make_async_copy(fields_ref.at[:, :, c], record_ref.at[:, :, c], arrived.at[i])
        for i, c in enumerate(chunks)
    ]
    small = [
        pltpu.make_async_copy(events_ref, own_events, arrived.at[len(chunks)]),
        pltpu.make_async_copy(days_ref, own_days, arrived.at[len(chunks) + 1]),
    ]
    for copy in small + copies:
        copy.start()
    for copy in small:
        copy.wait()
    left_factor(me_ref[0], own_events, own_days, left_ref)
    for v in range(2):
        left = left_ref[v * half : (v + 1) * half, :]
        pad = jnp.zeros((EXTRA - TILE, left.shape[1]), BF16)
        all_ref[v * half : (v + 1) * half, points:] = dot_nt(
            left, jnp.concatenate([left[rows:, :], pad], axis=0)
        )
    record = record_ref.reshape(2 * record_ref.shape[0], points)
    for copy, c in zip(copies, chunks):
        copy.wait()
        all_ref[:, c] = dot(left_ref[...], record[:, c])
    for r in (2, 1, 3, 0):
        for v in range(2):
            top = v * half + group * r
            out = outs[SIDE * v + r]
            if r:
                main = all_ref[top : top + group, :]
                aux = all_ref[v * half + rows : (v + 1) * half, :]
                encode(out, main, aux, members, total_days)
            else:
                out[:group, :] = all_ref[top : top + group, :]
                out[group:, :] = all_ref[v * half + rows : (v + 1) * half, :]
    for i in range(SIDE * SIDE):
        for v in range(2):
            place = i if v == 0 else i % SIDE * SIDE + i // SIDE
            top = v * half + TILE * place
            part_ref[2 * TILE * i + TILE * v : 2 * TILE * i + TILE * (v + 1), :] = lane_sum(
                all_ref[top : top + TILE, :points]
            )
    design = [lane_sum(all_ref[v * half + rows : (v + 1) * half, :points]) for v in range(2)]
    types = [
        part_ref[pl.ds(pl.multiple_of((e ^ me_ref[0]) * 2 * TILE, 2 * TILE), 2 * TILE), :]
        for e in range(SIDE * SIDE)
    ]
    totals = lax.dot_general(
        jnp.ones((8, 128), F32),
        jnp.concatenate(types + design, axis=0),
        (((1,), (1,)), ((), ())),
        precision=lax.Precision.HIGHEST,
        preferred_element_type=F32,
    )
    count = 2 * TILE
    last = totals[0:1, count * SIDE * SIDE :]
    for e in range(SIDE * SIDE):
        line = [totals[0:1, count * e : count * (e + 1)], last, jnp.zeros((1, 128 - 2 * count), F32)]
        sums_ref[e : e + 1, :] = jnp.concatenate(line, axis=1)


def vmem():
    return pl.BlockSpec(memory_space=pltpu.VMEM)


def products(me, events, days, fields):
    local_days, _, points = fields.shape
    types = events.shape[0]
    group = types * TILE // SIDE
    half = types * TILE + TILE
    columns = points + EXTRA
    kept = jax.ShapeDtypeStruct((group + TILE, columns), F32)
    message = jax.ShapeDtypeStruct((group + TILE, columns), jnp.int16)
    tm = lax.axis_size("tm")
    sums = jax.ShapeDtypeStruct((tm, 128), F32)
    return pl.pallas_call(
        lambda *refs: products_kernel(local_days * tm, *refs),
        in_specs=[
            pl.BlockSpec(memory_space=pltpu.SMEM),
            pl.BlockSpec(memory_space=pltpu.HBM),
            pl.BlockSpec(memory_space=pltpu.HBM),
            pl.BlockSpec(memory_space=pltpu.HBM),
        ],
        out_specs=[vmem()] * (2 * SIDE + 1),
        out_shape=([kept] + [message] * (SIDE - 1)) * 2 + [sums],
        scratch_shapes=[
            pltpu.VMEM(fields.shape, BF16),
            pltpu.VMEM((2 * half, 2 * local_days), BF16),
            pltpu.VMEM((2 * half, columns), F32),
            pltpu.VMEM((2 * types * TILE, 128), F32),
            pltpu.VMEM(events.shape, jnp.int32),
            pltpu.VMEM((1, local_days), jnp.int32),
            pltpu.SemaphoreType.DMA((points // CHUNK + 2,)),
        ],
        compiler_params=pltpu.CompilerParams(vmem_limit_bytes=PRODUCTS_VMEM),
        name="products",
    )(me, *(pltpu.with_memory_space_constraint(x, pltpu.HBM) for x in (events, days.reshape(1, local_days), fields)))


def added(taken, members, total_days):
    rows, points = taken[0].shape[0] - TILE, taken[0].shape[1] - EXTRA
    kept = taken[0]
    main, side = kept[:rows, :points], kept[:rows, points:]
    aux, low_side = kept[rows:, :points], kept[rows:, points:]
    for t in taken[1:]:
        a, b, c, d = decode(t, members, total_days)
        main, side, aux, low_side = main + a, side + b, aux + c, low_side + d
    main = jnp.concatenate([main, side], axis=1)
    aux = jnp.concatenate([aux, low_side], axis=1)
    return main, aux


def merge_kernel(members, total_days, *refs):
    taken, outs = refs[:SIDE], refs[SIDE:]
    main, aux = added(taken, members, total_days)
    for r in (2, 1, 3):
        encode(outs[r], main[TILE * r : TILE * (r + 1)], aux, members, total_days)
    outs[0][:TILE, :] = main[:TILE]
    outs[0][TILE:, :] = aux


def merge(taken, members, total_days):
    columns = taken[0].shape[1]
    kept = jax.ShapeDtypeStruct((2 * TILE, columns), F32)
    message = jax.ShapeDtypeStruct((2 * TILE, columns), jnp.int16)
    return pl.pallas_call(
        lambda *refs: merge_kernel(members, total_days, *refs),
        in_specs=[vmem()] * SIDE,
        out_specs=[vmem()] * SIDE,
        out_shape=[kept] + [message] * (SIDE - 1),
        compiler_params=pltpu.CompilerParams(vmem_limit_bytes=MERGE_VMEM),
        name="merge",
    )(*taken)


def finish_kernel(members, total_days, all_points, lags_ref, sums_ref, *refs):
    taken, (maps_ref, rows_ref) = refs[: 2 * SIDE], refs[2 * SIDE :]
    lags, _, points = maps_ref.shape
    sums = jnp.sum(sums_ref[...], axis=0, keepdims=True)
    for v in range(2):
        total = jnp.concatenate(added(taken[SIDE * v : SIDE * (v + 1)], members, total_days), axis=0)
        row, lane = iota((2 * TILE, 1), 0), iota((1, EXTRA), 1)
        place = jnp.where(row < TILE, row + TILE * v, row + TILE * (v + 1))
        over = jnp.where(iota((1, 128), 1) == place, sums, 0.0)
        over = jnp.sum(over, axis=1, keepdims=True)
        side = jnp.where(lane == CODE, over, total[:, points:])
        total = jnp.concatenate([total[:, :points], side], axis=1)
        for k in range(TERMS):
            pivot = total[TILE + k : TILE + k + 1, :]
            column = points + k
            factor = total[:, column : column + 1] / pivot[:, column : column + 1]
            factor = jnp.where((row < TILE) | (row > TILE + k), factor, 0.0)
            total = total - factor * pivot
        column = points + CODE
        mean = total[:TILE, column : column + 1] / all_points
        rows_ref[...] = (total[:TILE, :points] - mean) / members
        for l in range(lags):
            maps_ref[l, v : v + 1, :] = rows_ref[pl.ds(lags_ref[l], 1), :]


def finish(members, total_days, all_points, lag_offsets, sums, taken):
    points = taken[0].shape[1] - EXTRA
    lags = lag_offsets.shape[0]
    return pl.pallas_call(
        lambda *refs: finish_kernel(members, total_days, all_points, *refs),
        in_specs=[pl.BlockSpec(memory_space=pltpu.SMEM)] + [vmem()] * (2 * SIDE + 1),
        scratch_shapes=[pltpu.VMEM((TILE, points), F32)],
        out_shape=jax.ShapeDtypeStruct((lags, 2, points), F32),
        compiler_params=pltpu.CompilerParams(vmem_limit_bytes=MERGE_VMEM),
        name="finish",
    )(lag_offsets, sums, *taken)


def swap(value, axis, mask):
    return lax.ppermute(value, axis, [(i, i ^ mask) for i in range(lax.axis_size(axis))])


def map_sums(sums):
    types, space = sums.shape[0], lax.axis_size("space")
    chips = space // 2
    sums = jnp.broadcast_to(sums[:, None], (types, chips, sums.shape[1]))
    groups = [[2 * i + core for i in range(types * chips)] for core in range(2)]
    return lax.all_to_all(
        sums.reshape(types * chips, -1), ("tm", "space"), 0, 0, axis_index_groups=groups, tiled=True
    )


def shards(fields, calendar_day, events, lag_offsets):
    me = lax.axis_index("tm").astype(jnp.int32).reshape(1)
    members = events.shape[1]
    total_days = fields.shape[0] * lax.axis_size("tm")
    all_points = fields.shape[2] * lax.axis_size("space")
    *sent, sums = products(me, events, calendar_day, fields)
    sent, sums = lax.optimization_barrier((sent, sums + swap(sums, "space", 1)))
    mine = [[sent[0]] + [None] * 3, [sent[SIDE]] + [None] * 3]
    for r in (2, 1, 3):
        mine[0][r] = swap(sent[r], "tm", SIDE * r)
        mine[1][r] = swap(sent[SIDE + r], "tm", r)
    sums = map_sums(sums)
    taken = []
    for v in range(2):
        parts = merge(mine[v], members, total_days)
        taken += [parts[0]] + [swap(parts[r], "tm", r if v == 0 else SIDE * r) for r in (1, 2, 3)]
    return finish(members, total_days, all_points, lag_offsets, sums, taken)[None]


def solution(mesh):
    return jax.shard_map(
        shards,
        mesh=mesh,
        in_specs=(P("tm", None, "space"), P("tm"), P(), P()),
        out_specs=P("tm", None, None, "space"),
        check_vma=False,
    )
```

```python
import jax
import jax.numpy as jnp
from jax import lax
from jax.experimental import pallas as pl
from jax.experimental.pallas import tpu as pltpu
from jax.sharding import PartitionSpec as P

HARMONICS = 4
TWO_PI = 6.283185307179586
TERMS = 2 * HARMONICS + 1
SIDE = 4
TILE = 16
EXTRA = 128
CODE = 32
MERGE_VMEM, PRODUCTS_VMEM = 8 << 20, 24 << 20
CHUNK = 512
TOP = 32767.0
SECOND = 65534.0
F32 = jnp.float32
BF16 = jnp.bfloat16


def near(rank):
    return (rank & 1) * 4 + (rank >> 1)


def far(rank):
    return (rank & 1) * 12 + (rank >> 1) * 3


def iota(shape, axis):
    return lax.broadcasted_iota(jnp.int32, shape, axis)


def dot(a, b):
    return jnp.dot(a, b, preferred_element_type=F32)


def dot_nt(a, b):
    return lax.dot_general(a, b, (((1,), (1,)), ((), ())), preferred_element_type=F32)


def design_rows(days):
    count = days.shape[1]
    phases = days.astype(F32) * (TWO_PI / 365.25)
    row = iota((TILE, count), 0)
    angles = ((row + 1) // 2).astype(F32) * phases
    waves = jnp.where(row % 2 == 1, jnp.cos(angles), jnp.sin(angles))
    rows = jnp.where(row == 0, 1.0, jnp.where(row < TERMS, waves, 0.0))
    return rows.astype(BF16)


def left_factor(me, events_ref, days_ref, left_ref):
    types, members = events_ref.shape
    lags = TILE
    local_days = days_ref.shape[1]
    rows = types * lags
    window = local_days + 128
    events = events_ref[...] - (me * local_days - 128)
    spot = iota((types, window), 1)
    histogram = jnp.zeros((types, window), F32)
    for m in range(members):
        histogram = histogram + jnp.where(events[:, m : m + 1] == spot, 1.0, 0.0)
    counts = jnp.concatenate(
        [histogram[:, 128 - o : 128 - o + local_days].astype(BF16) for o in range(lags)], axis=0
    )
    design = design_rows(days_ref[...])
    out_row = iota((rows, rows), 0)
    in_row = iota((rows, rows), 1)
    first, second, lag = out_row // (SIDE * lags), out_row // lags % SIDE, out_row % lags
    for v in range(2):
        rank = near(first) ^ far(second) if v == 0 else far(first) ^ near(second)
        order = (in_row == lag * types + (rank ^ me)).astype(F32).astype(BF16)
        spread = (iota((128, 256), 1) == 2 * iota((128, 256), 0) + v).astype(F32).astype(BF16)
        top = v * (rows + TILE)
        ordered = dot(order, counts).astype(BF16)
        for b in range(local_days // 128):
            day = slice(128 * b, 128 * b + 128)
            to = slice(256 * b, 256 * b + 256)
            left_ref[top : top + rows, to] = dot(ordered[:, day], spread).astype(BF16)
            left_ref[top + rows : top + rows + TILE, to] = dot(design[:, day], spread).astype(BF16)


def lane_sum(block):
    parts = [block[:, c : c + 128] for c in range(0, block.shape[1], 128)]
    while len(parts) > 1:
        parts = [x + y for x, y in zip(parts[::2], parts[1::2])] + parts[len(parts) & ~1 :]
    return parts[0]


def to_words(value, unit):
    scaled = value * unit
    high = jnp.round(scaled)
    return high, jnp.round((scaled - high) * SECOND)


def row_unit(code):
    return jnp.exp2(code * (-1.0 / 16.0)) * TOP


def row_code(value):
    peak = jnp.max(jnp.abs(value), axis=1, keepdims=True)
    return jnp.ceil(16.0 * jnp.log2(jnp.maximum(peak, 1e-30))) + 1.0


def to_int16(value):
    return value.astype(jnp.int32).astype(jnp.int16)


def encode(out, main, aux, members, total_days):
    rows, points = main.shape[0], main.shape[1] - EXTRA
    lane = iota((1, EXTRA), 1)

    def extra(block, code, unit):
        high, low = to_words(block, unit)
        low = jnp.where((lane >= TILE) & (lane < 2 * TILE), pltpu.roll(low, TILE, 1), 0.0)
        return to_int16(jnp.where(lane < TILE, high, low) + jnp.where(lane == CODE, code, 0.0))

    constant = aux[0:1, :points]
    mean = constant / aux[0:1, points : points + 1]
    centred = main[:, :points] - main[:, points : points + 1] * mean
    code = row_code(centred)
    out[:rows, :points] = to_int16(jnp.round(centred * row_unit(code)))
    out[:rows, points:] = extra(main[:, points:], code, TOP / members)
    row = iota((TILE, 1), 0)
    harmonic = aux[:, :points] - aux[:, points : points + 1] * mean
    harmonic = jnp.where(row == 0, constant, harmonic)
    code = row_code(harmonic)
    high, low = to_words(constant, row_unit(code[0:1]))
    words = jnp.where(row == 0, high, jnp.round(harmonic * row_unit(code)))
    out[rows:, :points] = to_int16(jnp.where(row == TERMS, low, words))
    out[rows:, points:] = extra(aux[:, points:], code, TOP / total_days)


def decode(message, members, total_days):
    rows, points = message.shape[0] - TILE, message.shape[1] - EXTRA
    lane = iota((1, EXTRA), 1)

    def extra(block, unit):
        words = block + pltpu.roll(block, EXTRA - TILE, 1) * (1.0 / SECOND)
        return jnp.where(lane < TILE, words * (1.0 / unit), 0.0)

    def values(block):
        block = block.astype(jnp.int32).astype(F32)
        code = block[:, points + CODE : points + CODE + 1]
        return block[:, :points], block[:, points:], jnp.exp2(code * (1.0 / 16.0)) * (1.0 / TOP)

    words, behind, step = values(message[rows:])
    low_side = extra(behind, TOP / total_days)
    constant = (words[0:1] + words[TERMS : TERMS + 1] * (1.0 / SECOND)) * step[0:1]
    mean = constant / low_side[0:1, 0:1]
    row = iota((TILE, 1), 0)
    aux = words * step + low_side[:, 0:1] * mean
    aux = jnp.where(row == 0, constant, jnp.where(row < TERMS, aux, 0.0))
    words, behind, step = values(message[:rows])
    side = extra(behind, TOP / members)
    return words * step + side[:, 0:1] * mean, side, aux, low_side


def products_kernel(total_days, me_ref, events_ref, days_ref, fields_ref, *refs):
    outs, sums_ref = refs[:-8], refs[-8]
    record_ref, left_ref, all_ref, part_ref, own_events, own_days, arrived = refs[-7:]
    members = events_ref.shape[1]
    points = fields_ref.shape[2]
    group = outs[0].shape[0] - TILE
    rows = SIDE * group
    half = rows + TILE
    chunks = [slice(c, c + CHUNK) for c in range(0, points, CHUNK)]
    copies = [
        pltpu.make_async_copy(fields_ref.at[:, :, c], record_ref.at[:, :, c], arrived.at[i])
        for i, c in enumerate(chunks)
    ]
    small = [
        pltpu.make_async_copy(events_ref, own_events, arrived.at[len(chunks)]),
        pltpu.make_async_copy(days_ref, own_days, arrived.at[len(chunks) + 1]),
    ]
    for copy in small + copies:
        copy.start()
    for copy in small:
        copy.wait()
    left_factor(me_ref[0], own_events, own_days, left_ref)
    for v in range(2):
        left = left_ref[v * half : (v + 1) * half, :]
        pad = jnp.zeros((EXTRA - TILE, left.shape[1]), BF16)
        all_ref[v * half : (v + 1) * half, points:] = dot_nt(
            left, jnp.concatenate([left[rows:, :], pad], axis=0)
        )
    record = record_ref.reshape(2 * record_ref.shape[0], points)
    for copy, c in zip(copies, chunks):
        copy.wait()
        all_ref[:, c] = dot(left_ref[...], record[:, c])
    for r in (2, 1, 3, 0):
        for v in range(2):
            top = v * half + group * r
            out = outs[SIDE * v + r]
            if r:
                main = all_ref[top : top + group, :]
                aux = all_ref[v * half + rows : (v + 1) * half, :]
                encode(out, main, aux, members, total_days)
            else:
                out[:group, :] = all_ref[top : top + group, :]
                out[group:, :] = all_ref[v * half + rows : (v + 1) * half, :]
    for i in range(SIDE * SIDE):
        for v in range(2):
            place = i if v == 0 else i % SIDE * SIDE + i // SIDE
            top = v * half + TILE * place
            part_ref[2 * TILE * i + TILE * v : 2 * TILE * i + TILE * (v + 1), :] = lane_sum(
                all_ref[top : top + TILE, :points]
            )
    design = [lane_sum(all_ref[v * half + rows : (v + 1) * half, :points]) for v in range(2)]
    types = []
    for e in range(SIDE * SIDE):
        rank = e ^ me_ref[0]
        high, mixed = rank & 10, rank ^ (rank >> 1)
        place = (mixed & 1) * 8 + (mixed >> 2 & 1) * 4 + (high & 2) + (high >> 3)
        types.append(part_ref[pl.ds(pl.multiple_of(place * 2 * TILE, 2 * TILE), 2 * TILE), :])
    totals = lax.dot_general(
        jnp.ones((8, 128), F32),
        jnp.concatenate(types + design, axis=0),
        (((1,), (1,)), ((), ())),
        precision=lax.Precision.HIGHEST,
        preferred_element_type=F32,
    )
    count = 2 * TILE
    last = totals[0:1, count * SIDE * SIDE :]
    space = sums_ref.shape[0] // (SIDE * SIDE)
    for e in range(SIDE * SIDE):
        line = [totals[0:1, count * e : count * (e + 1)], last, jnp.zeros((1, 128 - 2 * count), F32)]
        line = jnp.broadcast_to(jnp.concatenate(line, axis=1), (space, 128))
        sums_ref[space * e : space * (e + 1), :] = line


def vmem():
    return pl.BlockSpec(memory_space=pltpu.VMEM)


def products(me, events, days, fields):
    local_days, _, points = fields.shape
    types = events.shape[0]
    group = types * TILE // SIDE
    half = types * TILE + TILE
    columns = points + EXTRA
    kept = jax.ShapeDtypeStruct((group + TILE, columns), F32)
    message = jax.ShapeDtypeStruct((group + TILE, columns), jnp.int16)
    tm = lax.axis_size("tm")
    sums = jax.ShapeDtypeStruct((tm * lax.axis_size("space"), 128), F32)
    return pl.pallas_call(
        lambda *refs: products_kernel(local_days * tm, *refs),
        in_specs=[
            pl.BlockSpec(memory_space=pltpu.SMEM),
            pl.BlockSpec(memory_space=pltpu.HBM),
            pl.BlockSpec(memory_space=pltpu.HBM),
            pl.BlockSpec(memory_space=pltpu.HBM),
        ],
        out_specs=[vmem()] * (2 * SIDE + 1),
        out_shape=([kept] + [message] * (SIDE - 1)) * 2 + [sums],
        scratch_shapes=[
            pltpu.VMEM(fields.shape, BF16),
            pltpu.VMEM((2 * half, 2 * local_days), BF16),
            pltpu.VMEM((2 * half, columns), F32),
            pltpu.VMEM((2 * types * TILE, 128), F32),
            pltpu.VMEM(events.shape, jnp.int32),
            pltpu.VMEM((1, local_days), jnp.int32),
            pltpu.SemaphoreType.DMA((points // CHUNK + 2,)),
        ],
        compiler_params=pltpu.CompilerParams(vmem_limit_bytes=PRODUCTS_VMEM),
        name="products",
    )(me, *(pltpu.with_memory_space_constraint(x, pltpu.HBM) for x in (events, days.reshape(1, local_days), fields)))


def added(taken, members, total_days):
    rows, points = taken[0].shape[0] - TILE, taken[0].shape[1] - EXTRA
    kept = taken[0]
    main, side = kept[:rows, :points], kept[:rows, points:]
    aux, low_side = kept[rows:, :points], kept[rows:, points:]
    for t in taken[1:]:
        a, b, c, d = decode(t, members, total_days)
        main, side, aux, low_side = main + a, side + b, aux + c, low_side + d
    main = jnp.concatenate([main, side], axis=1)
    aux = jnp.concatenate([aux, low_side], axis=1)
    return main, aux


def merge_kernel(members, total_days, *refs):
    taken, outs = refs[:SIDE], refs[SIDE:]
    main, aux = added(taken, members, total_days)
    for r in (2, 1, 3):
        encode(outs[r], main[TILE * r : TILE * (r + 1)], aux, members, total_days)
    outs[0][:TILE, :] = main[:TILE]
    outs[0][TILE:, :] = aux


def merge(taken, members, total_days):
    columns = taken[0].shape[1]
    kept = jax.ShapeDtypeStruct((2 * TILE, columns), F32)
    message = jax.ShapeDtypeStruct((2 * TILE, columns), jnp.int16)
    return pl.pallas_call(
        lambda *refs: merge_kernel(members, total_days, *refs),
        in_specs=[vmem()] * SIDE,
        out_specs=[vmem()] * SIDE,
        out_shape=[kept] + [message] * (SIDE - 1),
        compiler_params=pltpu.CompilerParams(vmem_limit_bytes=MERGE_VMEM),
        name="merge",
    )(*taken)


def fold_kernel(v, members, total_days, *refs):
    taken, rows_ref = refs[:SIDE], refs[SIDE]
    total = jnp.concatenate(added(taken, members, total_days), axis=0)
    points = total.shape[1] - EXTRA
    row, lane = iota((2 * TILE, 1), 0), iota((1, EXTRA), 1)
    unit = (lane == TILE * (v + 1) + row) & (row >= TILE) & (row < TILE + TERMS)
    total = jnp.concatenate([total[:, :points], jnp.where(unit, 1.0, total[:, points:])], axis=1)
    for k in range(TERMS):
        pivot = total[TILE + k : TILE + k + 1, :]
        column = points + k
        factor = total[:, column : column + 1] / pivot[:, column : column + 1]
        factor = jnp.where((row < TILE) | (row > TILE + k), factor, 0.0)
        total = total - factor * pivot
    rows_ref[...] = total[:TILE]


def fold(v, taken, members, total_days):
    return pl.pallas_call(
        lambda *refs: fold_kernel(v, members, total_days, *refs),
        in_specs=[vmem()] * SIDE,
        out_specs=vmem(),
        out_shape=jax.ShapeDtypeStruct((TILE, taken[0].shape[1]), F32),
        compiler_params=pltpu.CompilerParams(vmem_limit_bytes=MERGE_VMEM),
        name="fold",
    )(*taken)


def finish_kernel(members, all_points, lags_ref, sums_ref, *refs):
    folded, maps_ref, rows_ref = refs[:2], refs[2], refs[3]
    lags, _, points = maps_ref.shape
    sums = jnp.sum(sums_ref[...], axis=0, keepdims=True)
    row, lane = iota((TILE, 1), 0), iota((1, EXTRA), 1)
    for v in range(2):
        rows = folded[v][...]
        design = (lane >= TILE * (v + 2)) & (lane < TILE * (v + 3))
        weights = jnp.where(lane == TILE * v + row, 1.0, jnp.where(design, rows[:, points:], 0.0))
        mean = jnp.sum(weights * sums, axis=1, keepdims=True) / all_points
        rows_ref[...] = (rows[:, :points] - mean) / members
        for l in range(lags):
            maps_ref[l, v : v + 1, :] = rows_ref[pl.ds(lags_ref[l], 1), :]


def finish(members, all_points, lag_offsets, sums, folded):
    points = folded[0].shape[1] - EXTRA
    lags = lag_offsets.shape[0]
    return pl.pallas_call(
        lambda *refs: finish_kernel(members, all_points, *refs),
        in_specs=[pl.BlockSpec(memory_space=pltpu.SMEM)] + [vmem()] * 3,
        scratch_shapes=[pltpu.VMEM((TILE, points), F32)],
        out_shape=jax.ShapeDtypeStruct((lags, 2, points), F32),
        compiler_params=pltpu.CompilerParams(vmem_limit_bytes=MERGE_VMEM),
        name="finish",
    )(lag_offsets, sums, *folded)


def swap(value, axis, mask):
    return lax.ppermute(value, axis, [(i, i ^ mask) for i in range(lax.axis_size(axis))])


def shards(fields, calendar_day, events, lag_offsets):
    me = lax.axis_index("tm").astype(jnp.int32).reshape(1)
    members = events.shape[1]
    total_days = fields.shape[0] * lax.axis_size("tm")
    all_points = fields.shape[2] * lax.axis_size("space")
    *sent, sums = products(me, events, calendar_day, fields)
    mine = [[sent[0]] + [None] * 3, [sent[SIDE]] + [None] * 3]
    for r in (3, 1, 2):
        mine[0][r] = swap(sent[r], "tm", near(r))
        mine[1][r] = swap(sent[SIDE + r], "tm", far(r))
    sums = lax.all_to_all(sums, ("tm", "space"), 0, 0, tiled=True)
    folded = []
    for v in range(2):
        parts = merge(mine[v], members, total_days)
        got = [swap(parts[r], "tm", far(r) if v == 0 else near(r)) for r in (1, 2, 3)]
        folded.append(fold(v, [parts[0]] + got, members, total_days))
    return finish(members, all_points, lag_offsets, sums, folded)[None]


def solution(mesh):
    return jax.shard_map(
        shards,
        mesh=mesh,
        in_specs=(P("tm", None, "space"), P("tm"), P(), P()),
        out_specs=P("tm", None, None, "space"),
        check_vma=False,
    )
```

```python
import jax
import jax.numpy as jnp
from jax import lax
from jax.experimental import pallas as pl
from jax.experimental.pallas import tpu as pltpu
from jax.sharding import PartitionSpec as P

HARMONICS = 4
TWO_PI = 6.283185307179586
TERMS = 2 * HARMONICS + 1
SIDE = 4
TILE = 16
EXTRA = 128
CODE = 32
MERGE_VMEM, PRODUCTS_VMEM = 8 << 20, 24 << 20
CHUNK = 512
TOP = 32767.0
SECOND = 65534.0
F32 = jnp.float32
BF16 = jnp.bfloat16


def near(rank):
    return (rank & 1) * 4 + (rank >> 1)


def far(rank):
    return (rank & 1) * 12 + (rank >> 1) * 3


def iota(shape, axis):
    return lax.broadcasted_iota(jnp.int32, shape, axis)


def dot(a, b):
    return jnp.dot(a, b, preferred_element_type=F32)


def dot_nt(a, b):
    return lax.dot_general(a, b, (((1,), (1,)), ((), ())), preferred_element_type=F32)


def design_rows(days):
    count = days.shape[1]
    phases = days.astype(F32) * (TWO_PI / 365.25)
    row = iota((TILE, count), 0)
    angles = ((row + 1) // 2).astype(F32) * phases
    waves = jnp.where(row % 2 == 1, jnp.cos(angles), jnp.sin(angles))
    rows = jnp.where(row == 0, 1.0, jnp.where(row < TERMS, waves, 0.0))
    return rows.astype(BF16)


def left_factor(me, events_ref, days_ref, left_ref):
    types, members = events_ref.shape
    lags = TILE
    local_days = days_ref.shape[1]
    rows = types * lags
    window = local_days + 128
    events = events_ref[...] - (me * local_days - 128)
    spot = iota((types, window), 1)
    histogram = jnp.zeros((types, window), F32)
    for m in range(members):
        histogram = histogram + jnp.where(events[:, m : m + 1] == spot, 1.0, 0.0)
    counts = jnp.concatenate(
        [histogram[:, 128 - o : 128 - o + local_days].astype(BF16) for o in range(lags)], axis=0
    )
    design = design_rows(days_ref[...])
    out_row = iota((rows, rows), 0)
    in_row = iota((rows, rows), 1)
    first, second, lag = out_row // (SIDE * lags), out_row // lags % SIDE, out_row % lags
    for v in range(2):
        rank = near(first) ^ far(second) if v == 0 else far(first) ^ near(second)
        order = (in_row == lag * types + (rank ^ me)).astype(F32).astype(BF16)
        spread = (iota((128, 256), 1) == 2 * iota((128, 256), 0) + v).astype(F32).astype(BF16)
        top = v * (rows + TILE)
        ordered = dot(order, counts).astype(BF16)
        for b in range(local_days // 128):
            day = slice(128 * b, 128 * b + 128)
            to = slice(256 * b, 256 * b + 256)
            left_ref[top : top + rows, to] = dot(ordered[:, day], spread).astype(BF16)
            left_ref[top + rows : top + rows + TILE, to] = dot(design[:, day], spread).astype(BF16)


def lane_sum(block):
    parts = [block[:, c : c + 128] for c in range(0, block.shape[1], 128)]
    while len(parts) > 1:
        parts = [x + y for x, y in zip(parts[::2], parts[1::2])] + parts[len(parts) & ~1 :]
    return parts[0]


def to_words(value, unit):
    scaled = value * unit
    high = jnp.round(scaled)
    return high, jnp.round((scaled - high) * SECOND)


def row_unit(code):
    return jnp.exp2(code * (-1.0 / 16.0)) * TOP


def row_code(value):
    peak = jnp.max(jnp.abs(value), axis=1, keepdims=True)
    return jnp.ceil(16.0 * jnp.log2(jnp.maximum(peak, 1e-30))) + 1.0


def to_int16(value):
    return value.astype(jnp.int32).astype(jnp.int16)


def encode(out, main, aux, members, total_days):
    rows, points = main.shape[0], main.shape[1] - EXTRA
    lane = iota((1, EXTRA), 1)

    def extra(block, code, unit):
        high, low = to_words(block, unit)
        low = jnp.where((lane >= TILE) & (lane < 2 * TILE), pltpu.roll(low, TILE, 1), 0.0)
        return to_int16(jnp.where(lane < TILE, high, low) + jnp.where(lane == CODE, code, 0.0))

    constant = aux[0:1, :points]
    mean = constant / aux[0:1, points : points + 1]
    centred = main[:, :points] - main[:, points : points + 1] * mean
    code = row_code(centred)
    out[:rows, :points] = to_int16(jnp.round(centred * row_unit(code)))
    out[:rows, points:] = extra(main[:, points:], code, TOP / members)
    row = iota((TILE, 1), 0)
    harmonic = aux[:, :points] - aux[:, points : points + 1] * mean
    harmonic = jnp.where(row == 0, constant, harmonic)
    code = row_code(harmonic)
    high, low = to_words(constant, row_unit(code[0:1]))
    words = jnp.where(row == 0, high, jnp.round(harmonic * row_unit(code)))
    out[rows:, :points] = to_int16(jnp.where(row == TERMS, low, words))
    out[rows:, points:] = extra(aux[:, points:], code, TOP / total_days)


def decode(message, members, total_days):
    rows, points = message.shape[0] - TILE, message.shape[1] - EXTRA
    lane = iota((1, EXTRA), 1)

    def extra(block, unit):
        words = block + pltpu.roll(block, EXTRA - TILE, 1) * (1.0 / SECOND)
        return jnp.where(lane < TILE, words * (1.0 / unit), 0.0)

    def values(block):
        block = block.astype(jnp.int32).astype(F32)
        code = block[:, points + CODE : points + CODE + 1]
        return block[:, :points], block[:, points:], jnp.exp2(code * (1.0 / 16.0)) * (1.0 / TOP)

    words, behind, step = values(message[rows:])
    low_side = extra(behind, TOP / total_days)
    constant = (words[0:1] + words[TERMS : TERMS + 1] * (1.0 / SECOND)) * step[0:1]
    mean = constant / low_side[0:1, 0:1]
    row = iota((TILE, 1), 0)
    aux = words * step + low_side[:, 0:1] * mean
    aux = jnp.where(row == 0, constant, jnp.where(row < TERMS, aux, 0.0))
    words, behind, step = values(message[:rows])
    side = extra(behind, TOP / members)
    return words * step + side[:, 0:1] * mean, side, aux, low_side


def products_kernel(total_days, me_ref, events_ref, days_ref, fields_ref, *refs):
    outs, sums_ref = refs[:-8], refs[-8]
    record_ref, left_ref, all_ref, part_ref, own_events, own_days, arrived = refs[-7:]
    members = events_ref.shape[1]
    points = fields_ref.shape[2]
    group = outs[0].shape[0] - TILE
    rows = SIDE * group
    half = rows + TILE
    chunks = [slice(c, c + CHUNK) for c in range(0, points, CHUNK)]
    block = fields_ref.shape[0] // len(chunks)
    copies = [
        pltpu.make_async_copy(
            fields_ref.at[pl.ds(block * i, block)], record_ref.at[pl.ds(block * i, block)], arrived.at[i]
        )
        for i in range(len(chunks))
    ]
    small = [
        pltpu.make_async_copy(events_ref, own_events, arrived.at[len(chunks)]),
        pltpu.make_async_copy(days_ref, own_days, arrived.at[len(chunks) + 1]),
    ]
    for copy in small + copies:
        copy.start()
    for copy in small:
        copy.wait()
    left_factor(me_ref[0], own_events, own_days, left_ref)
    for v in range(2):
        left = left_ref[v * half : (v + 1) * half, :]
        pad = jnp.zeros((EXTRA - TILE, left.shape[1]), BF16)
        all_ref[v * half : (v + 1) * half, points:] = dot_nt(
            left, jnp.concatenate([left[rows:, :], pad], axis=0)
        )
    record = record_ref.reshape(2 * record_ref.shape[0], points)
    for copy in copies:
        copy.wait()
    for c in chunks:
        all_ref[:, c] = dot(left_ref[...], record[:, c])
    for r in (2, 1, 3, 0):
        for v in range(2):
            top = v * half + group * r
            out = outs[SIDE * v + r]
            if r:
                main = all_ref[top : top + group, :]
                aux = all_ref[v * half + rows : (v + 1) * half, :]
                encode(out, main, aux, members, total_days)
            else:
                out[:group, :] = all_ref[top : top + group, :]
                out[group:, :] = all_ref[v * half + rows : (v + 1) * half, :]
    for i in range(SIDE * SIDE):
        for v in range(2):
            place = i if v == 0 else i % SIDE * SIDE + i // SIDE
            top = v * half + TILE * place
            part_ref[2 * TILE * i + TILE * v : 2 * TILE * i + TILE * (v + 1), :] = lane_sum(
                all_ref[top : top + TILE, :points]
            )
    design = [lane_sum(all_ref[v * half + rows : (v + 1) * half, :points]) for v in range(2)]
    types = []
    for e in range(SIDE * SIDE):
        rank = e ^ me_ref[0]
        high, mixed = rank & 10, rank ^ (rank >> 1)
        place = (mixed & 1) * 8 + (mixed >> 2 & 1) * 4 + (high & 2) + (high >> 3)
        types.append(part_ref[pl.ds(pl.multiple_of(place * 2 * TILE, 2 * TILE), 2 * TILE), :])
    totals = lax.dot_general(
        jnp.ones((8, 128), F32),
        jnp.concatenate(types + design, axis=0),
        (((1,), (1,)), ((), ())),
        precision=lax.Precision.HIGHEST,
        preferred_element_type=F32,
    )
    count = 2 * TILE
    last = totals[0:1, count * SIDE * SIDE :]
    space = sums_ref.shape[0] // (SIDE * SIDE)
    for e in range(SIDE * SIDE):
        line = [totals[0:1, count * e : count * (e + 1)], last, jnp.zeros((1, 128 - 2 * count), F32)]
        line = jnp.broadcast_to(jnp.concatenate(line, axis=1), (space, 128))
        sums_ref[space * e : space * (e + 1), :] = line


def vmem():
    return pl.BlockSpec(memory_space=pltpu.VMEM)


def products(me, events, days, fields):
    local_days, _, points = fields.shape
    types = events.shape[0]
    group = types * TILE // SIDE
    half = types * TILE + TILE
    columns = points + EXTRA
    kept = jax.ShapeDtypeStruct((group + TILE, columns), F32)
    message = jax.ShapeDtypeStruct((group + TILE, columns), jnp.int16)
    tm = lax.axis_size("tm")
    sums = jax.ShapeDtypeStruct((tm * lax.axis_size("space"), 128), F32)
    return pl.pallas_call(
        lambda *refs: products_kernel(local_days * tm, *refs),
        in_specs=[
            pl.BlockSpec(memory_space=pltpu.SMEM),
            pl.BlockSpec(memory_space=pltpu.HBM),
            pl.BlockSpec(memory_space=pltpu.HBM),
            pl.BlockSpec(memory_space=pltpu.HBM),
        ],
        out_specs=[vmem()] * (2 * SIDE + 1),
        out_shape=([kept] + [message] * (SIDE - 1)) * 2 + [sums],
        scratch_shapes=[
            pltpu.VMEM(fields.shape, BF16),
            pltpu.VMEM((2 * half, 2 * local_days), BF16),
            pltpu.VMEM((2 * half, columns), F32),
            pltpu.VMEM((2 * types * TILE, 128), F32),
            pltpu.VMEM(events.shape, jnp.int32),
            pltpu.VMEM((1, local_days), jnp.int32),
            pltpu.SemaphoreType.DMA((points // CHUNK + 2,)),
        ],
        compiler_params=pltpu.CompilerParams(vmem_limit_bytes=PRODUCTS_VMEM),
        name="products",
    )(me, *(pltpu.with_memory_space_constraint(x, pltpu.HBM) for x in (events, days.reshape(1, local_days), fields)))


def added(taken, members, total_days):
    rows, points = taken[0].shape[0] - TILE, taken[0].shape[1] - EXTRA
    kept = taken[0]
    main, side = kept[:rows, :points], kept[:rows, points:]
    aux, low_side = kept[rows:, :points], kept[rows:, points:]
    for t in taken[1:]:
        a, b, c, d = decode(t, members, total_days)
        main, side, aux, low_side = main + a, side + b, aux + c, low_side + d
    main = jnp.concatenate([main, side], axis=1)
    aux = jnp.concatenate([aux, low_side], axis=1)
    return main, aux


def merge_kernel(members, total_days, *refs):
    for v in range(2):
        taken = refs[SIDE * v : SIDE * (v + 1)]
        outs = refs[SIDE * (v + 2) : SIDE * (v + 3)]
        main, aux = added(taken, members, total_days)
        for r in (3, 1, 2):
            encode(outs[r], main[TILE * r : TILE * (r + 1)], aux, members, total_days)
        outs[0][:TILE, :] = main[:TILE]
        outs[0][TILE:, :] = aux


def merge(taken, members, total_days):
    columns = taken[0].shape[1]
    kept = jax.ShapeDtypeStruct((2 * TILE, columns), F32)
    message = jax.ShapeDtypeStruct((2 * TILE, columns), jnp.int16)
    return pl.pallas_call(
        lambda *refs: merge_kernel(members, total_days, *refs),
        in_specs=[vmem()] * (2 * SIDE),
        out_specs=[vmem()] * (2 * SIDE),
        out_shape=([kept] + [message] * (SIDE - 1)) * 2,
        compiler_params=pltpu.CompilerParams(vmem_limit_bytes=MERGE_VMEM),
        name="merge",
    )(*taken)


def fold_kernel(v, members, total_days, *refs):
    taken, rows_ref = refs[:SIDE], refs[SIDE]
    total = jnp.concatenate(added(taken, members, total_days), axis=0)
    points = total.shape[1] - EXTRA
    row, lane = iota((2 * TILE, 1), 0), iota((1, EXTRA), 1)
    unit = (lane == TILE * (v + 1) + row) & (row >= TILE) & (row < TILE + TERMS)
    total = jnp.concatenate([total[:, :points], jnp.where(unit, 1.0, total[:, points:])], axis=1)
    for k in range(TERMS):
        pivot = total[TILE + k : TILE + k + 1, :]
        column = points + k
        factor = total[:, column : column + 1] / pivot[:, column : column + 1]
        factor = jnp.where((row < TILE) | (row > TILE + k), factor, 0.0)
        total = total - factor * pivot
    rows_ref[...] = total[:TILE]


def fold(v, taken, members, total_days):
    return pl.pallas_call(
        lambda *refs: fold_kernel(v, members, total_days, *refs),
        in_specs=[vmem()] * SIDE,
        out_specs=vmem(),
        out_shape=jax.ShapeDtypeStruct((TILE, taken[0].shape[1]), F32),
        compiler_params=pltpu.CompilerParams(vmem_limit_bytes=MERGE_VMEM),
        name="fold",
    )(*taken)


def finish_kernel(members, all_points, lags_ref, sums_ref, *refs):
    folded, maps_ref, rows_ref = refs[:2], refs[2], refs[3]
    lags, _, points = maps_ref.shape
    sums = jnp.sum(sums_ref[...], axis=0, keepdims=True)
    row, lane = iota((TILE, 1), 0), iota((1, EXTRA), 1)
    for v in range(2):
        rows = folded[v][...]
        design = (lane >= TILE * (v + 2)) & (lane < TILE * (v + 3))
        weights = jnp.where(lane == TILE * v + row, 1.0, jnp.where(design, rows[:, points:], 0.0))
        mean = jnp.sum(weights * sums, axis=1, keepdims=True) / all_points
        rows_ref[...] = (rows[:, :points] - mean) / members
        for l in range(lags):
            maps_ref[l, v : v + 1, :] = rows_ref[pl.ds(lags_ref[l], 1), :]


def finish(members, all_points, lag_offsets, sums, folded):
    points = folded[0].shape[1] - EXTRA
    lags = lag_offsets.shape[0]
    return pl.pallas_call(
        lambda *refs: finish_kernel(members, all_points, *refs),
        in_specs=[pl.BlockSpec(memory_space=pltpu.SMEM)] + [vmem()] * 3,
        scratch_shapes=[pltpu.VMEM((TILE, points), F32)],
        out_shape=jax.ShapeDtypeStruct((lags, 2, points), F32),
        compiler_params=pltpu.CompilerParams(vmem_limit_bytes=MERGE_VMEM),
        name="finish",
    )(lag_offsets, sums, *folded)


def swap(value, axis, mask):
    return lax.ppermute(value, axis, [(i, i ^ mask) for i in range(lax.axis_size(axis))])


def shards(fields, calendar_day, events, lag_offsets):
    me = lax.axis_index("tm").astype(jnp.int32).reshape(1)
    members = events.shape[1]
    total_days = fields.shape[0] * lax.axis_size("tm")
    all_points = fields.shape[2] * lax.axis_size("space")
    *sent, sums = products(me, events, calendar_day, fields)
    mine = [[sent[0]] + [None] * 3, [sent[SIDE]] + [None] * 3]
    for r in (3, 1, 2):
        mine[0][r] = swap(sent[r], "tm", near(r))
        mine[1][r] = swap(sent[SIDE + r], "tm", far(r))
    sums = lax.all_to_all(sums, ("tm", "space"), 0, 0, tiled=True)
    parts = merge(mine[0] + mine[1], members, total_days)
    got = [[parts[0]] + [None] * 3, [parts[SIDE]] + [None] * 3]
    for r in (3, 1, 2):
        got[0][r] = swap(parts[r], "tm", far(r))
        got[1][r] = swap(parts[SIDE + r], "tm", near(r))
    folded = [fold(v, got[v], members, total_days) for v in range(2)]
    return finish(members, all_points, lag_offsets, sums, folded)[None]


def solution(mesh):
    return jax.shard_map(
        shards,
        mesh=mesh,
        in_specs=(P("tm", None, "space"), P("tm"), P(), P()),
        out_specs=P("tm", None, None, "space"),
        check_vma=False,
    )
```
